32 devices in a mesh: cuts: 2 (over y), vec: 4 (over z), space: 2 (over x), rep: 2 (over core).
Axes of the slice: x: 2, y: 2, z: 4, core: 2. Of those that a mesh axis runs over, the one named last changes fastest.
Arguments:
- colour_vectors: float32 [256, 2, 3, 6, 2304], P(('cuts', 'vec'), None, None, 'space', 'rep'), parts along dimension 0, may hold values from -6 to 6
- gauge_links: float32 [3, 2, 3, 3, 12, 2304], P(None, None, None, None, ('cuts', 'space'), 'rep'), parts along dimension 4, may hold values from -1 to 1, as said below
Outputs:
- filtered: float32 [256, 2, 3, 6, 2304], P(('cuts', 'vec'), None, None, 'space', 'rep'), parts along dimension 0
- gram_matrix: float32 [2, 256, 128], P(None, ('cuts', 'vec')), parts along dimension 1
- projected: float32 [2, 256, 128], P(None, ('cuts', 'vec')), parts along dimension 1
The draws below stay inside these ranges and needn't reach their ends.
There are 2 independent parts, one for each index of `cuts`. The reference program is written for one: setup_inputs(seed, part) draws one part's arguments, and reference() takes and returns one part's arrays. A program takes and returns all parts, laid end to end along the dimension named above; each array names one. Nothing has to cross between parts.
Inputs may be any that keep to these rules, and one draw needn't show every extreme that they name: `gauge_links`: each link is a unitary 3 x 3 complex matrix.
All inputs are finite; a program needn't handle non-finite values.
Results may differ from the reference program's by a relative error of at most 0.00017.
Values sent between devices are 32-bit elements; how exact they have to be, the bound alone decides.
A program may use at most 128 MiB of HBM per device.

```python
import math
from functools import partial
import jax
import jax.numpy as jnp
from jax import lax

NVEC = 128
LX = 48
LY = 48
DEG = 8
NZ = 6


def matrix_product(left_matrix, right_matrix):
    return [[left_matrix[row_index][0] * right_matrix[0][col_index] + left_matrix[row_index][1] * right_matrix[1][col_index] + left_matrix[row_index][2] * right_matrix[2][col_index] for col_index in range(3)] for row_index in range(3)]


def draw_gauge_links(key, part):
    angle_key = jax.random.fold_in(key, 11)
    phase_key = jax.random.fold_in(key, 23)
    field_shape = (3, NZ, LX * LY)
    angles = jax.random.uniform(angle_key, (3,) + field_shape, jnp.float32, 0.0, 2.0 * math.pi)
    phases = jax.random.uniform(phase_key, (6,) + field_shape, jnp.float32, -math.pi, math.pi)
    cosine_values = jnp.cos(angles)
    sine_values = jnp.sin(angles)
    ones_field = jnp.ones(field_shape, jnp.float32)
    zeros_field = jnp.zeros(field_shape, jnp.float32)
    first_turn = [[cosine_values[0], -sine_values[0], zeros_field], [sine_values[0], cosine_values[0], zeros_field], [zeros_field, zeros_field, ones_field]]
    second_turn = [[cosine_values[1], zeros_field, -sine_values[1]], [zeros_field, ones_field, zeros_field], [sine_values[1], zeros_field, cosine_values[1]]]
    third_turn = [[ones_field, zeros_field, zeros_field], [zeros_field, cosine_values[2], -sine_values[2]], [zeros_field, sine_values[2], cosine_values[2]]]
    orthogonal = matrix_product(matrix_product(first_turn, second_turn), third_turn)
    real_part = jnp.stack([jnp.stack([orthogonal[row_index][col_index] * jnp.cos(phases[row_index] + phases[3 + col_index]) for col_index in range(3)]) for row_index in range(3)])
    imag_part = jnp.stack([jnp.stack([orthogonal[row_index][col_index] * jnp.sin(phases[row_index] + phases[3 + col_index]) for col_index in range(3)]) for row_index in range(3)])
    whole_links = jnp.stack([real_part, imag_part])
    return jnp.transpose(whole_links, (3, 0, 1, 2, 4, 5))


def block_levels(stream_key, shape, split, smallest, largest):
    loudness = 1.0
    for dim, parts in split:
        heights = jax.random.uniform(jax.random.fold_in(jax.random.fold_in(stream_key, 6), dim), (parts,), jnp.float32, smallest / len(split), largest / len(split))
        loudness = loudness * jnp.repeat(jnp.exp(heights), shape[dim] // parts).reshape((-1,) + (1,) * (len(shape) - 1 - dim))
    return loudness


def centred(key, shape, spread, bound, pieces=(), kind=jnp.bfloat16):
    result = jax.random.normal(key, shape, jnp.float32) * spread
    if len(pieces) > 0:
        result = block_levels(key, shape, pieces, -0.22, 0.18) * result
    return jnp.clip(result, min=-bound, max=bound).astype(kind)


def setup_inputs(seed: int = 0, part: int = 0) -> dict:
    splits = jax.random.split(jax.random.key(seed), 3)
    own_keys = jax.random.split(jax.random.fold_in(splits[2], part), 3)
    return {
        "colour_vectors": centred(own_keys[0], (NVEC, 2, 3, NZ, LX * LY), 1.0, 6.0, ((0, 4), (3, 2), (4, 2)), jnp.float32),
        "gauge_links": draw_gauge_links(jax.random.fold_in(jax.random.fold_in(splits[2], part), 71), part),
    }


def apply_link(link, source, dagger):
    link_real = link[0]
    link_imag = link[1]
    vec_real = source[:, 0]
    vec_imag = source[:, 1]
    out_real = jnp.zeros_like(vec_real)
    out_imag = jnp.zeros_like(vec_imag)
    for column in range(3):
        if dagger:
            mat_real = link_real[column]
            mat_imag = -link_imag[column]
        else:
            mat_real = link_real[:, column]
            mat_imag = link_imag[:, column]
        src_real = vec_real[:, column][:, None]
        src_imag = vec_imag[:, column][:, None]
        out_real = out_real + (mat_real[None] * src_real - mat_imag[None] * src_imag)
        out_imag = out_imag + (mat_real[None] * src_imag + mat_imag[None] * src_real)
    return jnp.stack([out_real, out_imag], axis=1)


def hopping(source, gauge_links):
    positions = jnp.arange(source.shape[-1], dtype=jnp.int32) % LY
    last_y = positions == LY - 1
    first_y = positions == 0
    summed = apply_link(gauge_links[0], jnp.roll(source, -LY, -1), False) + jnp.roll(apply_link(gauge_links[0], source, True), LY, -1)
    ahead_y = jnp.where(last_y, jnp.roll(source, LY - 1, -1), jnp.roll(source, -1, -1))
    summed = summed + apply_link(gauge_links[1], ahead_y, False)
    backward_y = apply_link(gauge_links[1], source, True)
    summed = summed + jnp.where(first_y, jnp.roll(backward_y, 1 - LY, -1), jnp.roll(backward_y, 1, -1))
    summed = summed + apply_link(gauge_links[2], jnp.roll(source, -1, 3), False) + jnp.roll(apply_link(gauge_links[2], source, True), 1, 3)
    return summed


def filter_block(block_vectors, gauge_links):
    def filter_map(source):
        return -(source + 2.0 * hopping(source, gauge_links)) / 11.0

    previous = block_vectors
    current = filter_map(previous)
    for degree in range(DEG - 1):
        following = 2.0 * filter_map(current) - previous
        previous = current
        current = following
    laplace_image = 6.0 * current - hopping(current, gauge_links)
    return current, laplace_image


def inner_product(left_matrix, right_matrix):
    return lax.dot_general(left_matrix, right_matrix, (((1,), (1,)), ((), ())), precision=lax.Precision.HIGHEST, preferred_element_type=jnp.float32)


def block_pair(left_field, right_field):
    left_real = left_field[:, 0].reshape(left_field.shape[0], -1)
    left_imag = left_field[:, 1].reshape(left_field.shape[0], -1)
    right_real = right_field[:, 0].reshape(right_field.shape[0], -1)
    right_imag = right_field[:, 1].reshape(right_field.shape[0], -1)
    real_part = inner_product(left_real, right_real) + inner_product(left_imag, right_imag)
    imag_part = inner_product(left_real, right_imag) - inner_product(left_imag, right_real)
    return jnp.stack([real_part, imag_part])


def reference(colour_vectors, gauge_links):
    blocks = colour_vectors.reshape(NVEC // 8, 8, 2, 3, NZ, LX * LY)
    filtered, laplace_image = lax.map(partial(filter_block, gauge_links=gauge_links), blocks)
    filtered = filtered.reshape(NVEC, 2, 3, NZ, LX * LY)
    laplace_image = laplace_image.reshape(NVEC, 2, 3, NZ, LX * LY)
    site_count = float(LX * LY * NZ)
    gram_matrix = block_pair(filtered, filtered) / site_count
    projected = block_pair(filtered, laplace_image) / site_count
    return (filtered, gram_matrix, projected)
```

```python
import functools

import jax
import jax.numpy as jnp
from jax import lax
from jax.experimental import pallas as pl
from jax.experimental.pallas import tpu as pltpu
from jax.sharding import PartitionSpec as P

LX = 48
LY = 48
DEG = 8
LANES = 128


def shift_y(block, forward):
    width = block.shape[-1]
    position = lax.broadcasted_iota(jnp.int32, block.shape, 1) % LY
    if forward:
        return jnp.where(
            position == LY - 1,
            pltpu.roll(block, LY - 1, 1),
            pltpu.roll(block, width - 1, 1),
        )
    return jnp.where(
        position == 0, pltpu.roll(block, width - LY + 1, 1), pltpu.roll(block, 1, 1)
    )


def shift_x(block, forward):
    width = block.shape[-1]
    return pltpu.roll(block, width - LY if forward else LY, 1)


def prepare_links(links_ref, made_ref, planes):
    def one(z, carry):
        for mu in range(3):
            real = links_ref[z, mu * 2]
            imag = links_ref[z, mu * 2 + 1]
            sources = [(mu, real, imag)]
            if mu == 0:
                sources.append((3, shift_x(real, False), shift_x(imag, False)))
            if mu == 1:
                sources.append((4, shift_y(real, False), shift_y(imag, False)))
            for slot, a, b in sources:
                made_ref[z, slot * 3] = a
                made_ref[z, slot * 3 + 1] = b - a
                made_ref[z, slot * 3 + 2] = a + b
        return carry

    lax.fori_loop(0, planes, one, 0)


def hop_pass(source_ref, made_ref, moved_ref, planes, width, emit):
    def plane(z, carry):
        def move(comp, inner):
            field = source_ref[comp * planes + z]
            moved_ref[comp] = shift_x(field, True)
            moved_ref[6 + comp] = shift_y(field, True)
            moved_ref[12 + comp] = shift_x(field, False)
            moved_ref[18 + comp] = shift_y(field, False)
            return inner

        lax.fori_loop(0, 6, move, 0)
        ahead = lax.rem(z + 1, planes)
        behind = lax.rem(z + planes - 1, planes)

        def chunk(j, inner):
            lanes = pl.ds(pl.multiple_of(j * LANES, LANES), LANES)
            one = [None] * 3
            two = [None] * 3
            three = [None] * 3

            def add(total, term):
                return term if total is None else total + term

            def sub(total, term):
                return -term if total is None else total - term

            terms = (
                (0, z, lambda c: moved_ref[c, :, lanes], False),
                (1, z, lambda c: moved_ref[6 + c, :, lanes], False),
                (2, z, lambda c: source_ref[c * planes + ahead, :, lanes], False),
                (3, z, lambda c: moved_ref[12 + c, :, lanes], True),
                (4, z, lambda c: moved_ref[18 + c, :, lanes], True),
                (2, behind, lambda c: source_ref[c * planes + behind, :, lanes], True),
            )
            for slot, link_plane, load, dagger in terms:
                for col in range(3):
                    x = load(col)
                    y = load(3 + col)
                    both = x + y
                    for row in range(3):
                        entry = col * 3 + row if dagger else row * 3 + col
                        at = slice(entry, entry + 1)
                        a = made_ref[link_plane, slot * 3, at, lanes]
                        m = made_ref[link_plane, slot * 3 + 1, at, lanes]
                        p = made_ref[link_plane, slot * 3 + 2, at, lanes]
                        one[row] = add(one[row], a * both)
                        if dagger:
                            two[row] = sub(two[row], p * x)
                            three[row] = sub(three[row], m * y)
                        else:
                            two[row] = add(two[row], m * x)
                            three[row] = add(three[row], p * y)
            for row in range(3):
                emit(row * planes + z, lanes, one[row] - three[row])
                emit((3 + row) * planes + z, lanes, one[row] + two[row])
            return inner

        lax.fori_loop(0, width // LANES, chunk, 0)
        return carry

    lax.fori_loop(0, planes, plane, 0)


def filter_kernel(planes, width, start_ref, links_ref, out_ref, made_ref, fields_ref, moved_ref):
    prepare_links(links_ref, made_ref, planes)

    def fill(i, carry):
        fields_ref[0, i] = start_ref[i]
        fields_ref[1, i] = jnp.zeros_like(start_ref[i])
        return carry

    lax.fori_loop(0, 6 * planes, fill, 0)

    def step(k, carry):
        now = lax.rem(k, 2)
        later = 1 - now
        scale = jnp.where(k == 0, -1.0 / 11.0, -2.0 / 11.0).astype(jnp.float32)
        current = fields_ref.at[now]
        target = fields_ref.at[later]

        def emit(i, lanes, hop):
            target[i, :, lanes] = scale * (current[i, :, lanes] + 2.0 * hop) - target[i, :, lanes]

        hop_pass(current, made_ref, moved_ref, planes, width, emit)
        return carry

    lax.fori_loop(0, DEG, step, 0)

    def leave(i, carry):
        out_ref[i] = fields_ref[DEG % 2, i]
        return carry

    lax.fori_loop(0, 6 * planes, leave, 0)


def image_kernel(planes, width, field_ref, links_ref, out_ref, made_ref, moved_ref):
    prepare_links(links_ref, made_ref, planes)

    def emit(i, lanes, hop):
        out_ref[i, :, lanes] = 6.0 * field_ref[i, :, lanes] - hop

    hop_pass(field_ref, made_ref, moved_ref, planes, width, emit)


def run_kernel(kernel, field, links, planes, with_fields):
    _, count, width = field.shape
    scratch = [pltpu.VMEM((planes, 15, 9, width), jnp.float32)]
    if with_fields:
        scratch.append(pltpu.VMEM((2,) + field.shape, jnp.float32))
    scratch.append(pltpu.VMEM((24, count, width), jnp.float32))
    return pl.pallas_call(
        functools.partial(kernel, planes, width),
        out_shape=jax.ShapeDtypeStruct(field.shape, jnp.float32),
        in_specs=[pl.BlockSpec(memory_space=pltpu.VMEM)] * 2,
        out_specs=pl.BlockSpec(memory_space=pltpu.VMEM),
        scratch_shapes=scratch,
        compiler_params=pltpu.CompilerParams(vmem_limit_bytes=60 * 1024 * 1024),
    )(field, links)


def inner_product(left_matrix, right_matrix):
    return lax.dot_general(
        left_matrix,
        right_matrix,
        (((1,), (1,)), ((), ())),
        precision=lax.Precision.HIGH,
        preferred_element_type=jnp.float32,
    )


def body(colour_vectors, gauge_links):
    local_count, _, _, local_z, local_x = colour_vectors.shape
    space = lax.axis_size("space")
    rep = lax.axis_size("rep")
    group = space * rep
    count = local_count // group
    planes = local_z * space
    width = local_x * rep
    both = ("space", "rep")

    links = lax.all_gather(gauge_links, "space", axis=4, tiled=True)
    links = lax.all_gather(links, "rep", axis=5, tiled=True)
    links = links.reshape(6, 9, planes, width).transpose(2, 0, 1, 3)

    start = lax.all_to_all(
        colour_vectors.reshape(space, rep, count, 6, local_z, local_x).reshape(
            group, count, 6, local_z, local_x
        ),
        both,
        0,
        0,
    )
    start = start.reshape(space, rep, count, 6, local_z, local_x)
    start = start.transpose(3, 0, 4, 2, 1, 5).reshape(6 * planes, count, width)

    def home(field):
        field = field.reshape(6, space, local_z, count, rep, local_x)
        field = field.transpose(1, 4, 3, 0, 2, 5).reshape(group, count, 6, local_z, local_x)
        field = lax.all_to_all(field, both, 0, 0)
        return field.reshape(local_count, 2, 3, local_z, local_x)

    whole_filtered = run_kernel(filter_kernel, start, links, planes, True)
    filtered = home(whole_filtered)
    whole_image = run_kernel(image_kernel, whole_filtered, links, planes, False)
    image = home(whole_image)

    site_count = float(width * planes)
    panel = filtered.reshape(local_count, 2, -1)
    panels = lax.all_gather(panel, "vec", axis=0, tiled=True)
    rows = jnp.concatenate([panel, image.reshape(local_count, 2, -1)], axis=0)

    real_part = inner_product(rows[:, 0], panels[:, 0]) + inner_product(rows[:, 1], panels[:, 1])
    imag_part = inner_product(rows[:, 0], panels[:, 1]) - inner_product(rows[:, 1], panels[:, 0])
    result = lax.psum(jnp.stack([real_part, imag_part]), both) / site_count
    return (filtered, result[:, :local_count], result[:, local_count:])


def solution(mesh):
    return jax.shard_map(
        body,
        mesh=mesh,
        in_specs=(
            P(("cuts", "vec"), None, None, "space", "rep"),
            P(None, None, None, None, ("cuts", "space"), "rep"),
        ),
        out_specs=(
            P(("cuts", "vec"), None, None, "space", "rep"),
            P(None, ("cuts", "vec"), None),
            P(None, ("cuts", "vec"), None),
        ),
        check_vma=False,
    )
```

```python
import functools

import jax
import jax.numpy as jnp
from jax import lax
from jax.experimental import pallas as pl
from jax.experimental.pallas import tpu as pltpu
from jax.sharding import PartitionSpec as P

LX = 48
LY = 48
DEG = 8
LANES = 128


def shift_y(block, forward):
    width = block.shape[-1]
    position = lax.broadcasted_iota(jnp.int32, block.shape, 1) % LY
    if forward:
        return jnp.where(
            position == LY - 1,
            pltpu.roll(block, LY - 1, 1),
            pltpu.roll(block, width - 1, 1),
        )
    return jnp.where(
        position == 0, pltpu.roll(block, width - LY + 1, 1), pltpu.roll(block, 1, 1)
    )


def shift_x(block, forward):
    width = block.shape[-1]
    return pltpu.roll(block, width - LY if forward else LY, 1)


def piece_origin(piece, space, rep):
    i, j = piece // rep, piece % rep
    return (
        lax.rem(lax.axis_index("space") + space - i, space),
        lax.rem(lax.axis_index("rep") + rep - j, rep),
    )


def lane_block(index, size):
    return pl.ds(pl.multiple_of(index * size, LANES), size)


def prepare_links(pieces, made_ref, space, rep):
    local_z, _, _, local_x = pieces[0].shape
    for number, piece in enumerate(pieces):
        origin, half = piece_origin(number, space, rep)

        def place(z, carry, piece=piece, origin=origin, half=half):
            for mu in range(3):
                for part in range(2):
                    made_ref[origin * local_z + z, mu * 3 + part, :, lane_block(half, local_x)] = (
                        piece[z, mu * 2 + part]
                    )
            return carry

        lax.fori_loop(0, local_z, place, 0)

    def one(z, carry):
        for mu in range(3):
            real = made_ref[z, mu * 3]
            imag = made_ref[z, mu * 3 + 1]
            sources = [(mu, real, imag)]
            if mu == 0:
                sources.append((3, shift_x(real, False), shift_x(imag, False)))
            if mu == 1:
                sources.append((4, shift_y(real, False), shift_y(imag, False)))
            for slot, a, b in sources:
                made_ref[z, slot * 3] = a
                made_ref[z, slot * 3 + 1] = b - a
                made_ref[z, slot * 3 + 2] = a + b
        return carry

    lax.fori_loop(0, local_z * space, one, 0)


def hop_pass(source_ref, made_ref, moved_ref, planes, width, emit):
    def plane(z, carry):
        def move(comp, inner):
            field = source_ref[comp * planes + z]
            moved_ref[comp] = shift_x(field, True)
            moved_ref[6 + comp] = shift_y(field, True)
            moved_ref[12 + comp] = shift_x(field, False)
            moved_ref[18 + comp] = shift_y(field, False)
            return inner

        lax.fori_loop(0, 6, move, 0)
        ahead = lax.rem(z + 1, planes)
        behind = lax.rem(z + planes - 1, planes)

        def chunk(j, inner):
            lanes = pl.ds(pl.multiple_of(j * LANES, LANES), LANES)
            one = [None] * 3
            two = [None] * 3
            three = [None] * 3

            def add(total, term):
                return term if total is None else total + term

            def sub(total, term):
                return -term if total is None else total - term

            terms = (
                (0, z, lambda c: moved_ref[c, :, lanes], False),
                (1, z, lambda c: moved_ref[6 + c, :, lanes], False),
                (2, z, lambda c: source_ref[c * planes + ahead, :, lanes], False),
                (3, z, lambda c: moved_ref[12 + c, :, lanes], True),
                (4, z, lambda c: moved_ref[18 + c, :, lanes], True),
                (2, behind, lambda c: source_ref[c * planes + behind, :, lanes], True),
            )
            for slot, link_plane, load, dagger in terms:
                for col in range(3):
                    x = load(col)
                    y = load(3 + col)
                    both = x + y
                    for row in range(3):
                        entry = col * 3 + row if dagger else row * 3 + col
                        at = slice(entry, entry + 1)
                        a = made_ref[link_plane, slot * 3, at, lanes]
                        m = made_ref[link_plane, slot * 3 + 1, at, lanes]
                        p = made_ref[link_plane, slot * 3 + 2, at, lanes]
                        one[row] = add(one[row], a * both)
                        if dagger:
                            two[row] = sub(two[row], p * x)
                            three[row] = sub(three[row], m * y)
                        else:
                            two[row] = add(two[row], m * x)
                            three[row] = add(three[row], p * y)
            for row in range(3):
                emit(row * planes + z, lanes, one[row] - three[row])
                emit((3 + row) * planes + z, lanes, one[row] + two[row])
            return inner

        lax.fori_loop(0, width // LANES, chunk, 0)
        return carry

    lax.fori_loop(0, planes, plane, 0)


def filter_kernel(space, rep, *refs):
    group = space * rep
    starts, links = refs[:group], refs[group : 2 * group]
    out_ref, made_ref, fields_ref, moved_ref = refs[2 * group :]
    _, local_z, count, local_x = starts[0].shape
    planes = local_z * space
    width = local_x * rep
    prepare_links(links, made_ref, space, rep)

    for number, piece in enumerate(starts):
        origin, half = piece_origin(number, space, rep)

        def place(comp, carry, piece=piece, origin=origin, half=half):
            for z in range(local_z):
                at = comp * planes + origin * local_z + z
                block = piece[comp, z]
                fields_ref[0, at, :, lane_block(half, local_x)] = block
                fields_ref[1, at, :, lane_block(half, local_x)] = jnp.zeros_like(block)
            return carry

        lax.fori_loop(0, 6, place, 0)

    def step(k, carry):
        now = lax.rem(k, 2)
        later = 1 - now
        scale = jnp.where(k == 0, -1.0 / 11.0, -2.0 / 11.0).astype(jnp.float32)
        current = fields_ref.at[now]
        target = fields_ref.at[later]

        def emit(i, lanes, hop):
            target[i, :, lanes] = scale * (current[i, :, lanes] + 2.0 * hop) - target[i, :, lanes]

        hop_pass(current, made_ref, moved_ref, planes, width, emit)
        return carry

    lax.fori_loop(0, DEG, step, 0)

    def leave(i, carry):
        out_ref[i] = fields_ref[DEG % 2, i]
        return carry

    lax.fori_loop(0, 6 * planes, leave, 0)


def image_kernel(space, rep, *refs):
    group = space * rep
    field_ref, links = refs[0], refs[1 : 1 + group]
    out_ref, made_ref, moved_ref = refs[1 + group :]
    prepare_links(links, made_ref, space, rep)

    def emit(i, lanes, hop):
        out_ref[i, :, lanes] = 6.0 * field_ref[i, :, lanes] - hop

    hop_pass(field_ref, made_ref, moved_ref, field_ref.shape[0] // 6, field_ref.shape[2], emit)


def run_kernel(kernel, fields, links, shape, space, rep, hops):
    rows, count, width = shape
    scratch = [pltpu.VMEM((rows // 6, 15, 9, width), jnp.float32)]
    if hops > 1:
        scratch.append(pltpu.VMEM((2,) + shape, jnp.float32))
    scratch.append(pltpu.VMEM((24, count, width), jnp.float32))
    return pl.pallas_call(
        functools.partial(kernel, space, rep),
        out_shape=jax.ShapeDtypeStruct(shape, jnp.float32),
        in_specs=[pl.BlockSpec(memory_space=pltpu.VMEM)] * (len(fields) + len(links)),
        out_specs=pl.BlockSpec(memory_space=pltpu.VMEM),
        scratch_shapes=scratch,
        compiler_params=pltpu.CompilerParams(vmem_limit_bytes=62 * 1024 * 1024),
        cost_estimate=pl.CostEstimate(
            flops=hops * rows * count * width * 72, bytes_accessed=hops * 40_000_000, transcendentals=0
        ),
    )(*fields, *links)


def inner_product(left_matrix, right_matrix):
    return lax.dot_general(
        left_matrix,
        right_matrix,
        (((1,), (1,)), ((), ())),
        precision=lax.Precision.HIGH,
        preferred_element_type=jnp.float32,
    )


def from_behind(block, axis, distance):
    if distance == 0:
        return block
    count = lax.axis_size(axis)
    return lax.ppermute(block, axis, [(i, (i + distance) % count) for i in range(count)])


def exchange(blocks, space, rep):
    group = space * rep
    mine_space, mine_rep = lax.axis_index("space"), lax.axis_index("rep")
    received = []
    for piece in range(group):
        i, j = piece // rep, piece % rep
        to = lax.rem(mine_space + i, space) * rep + lax.rem(mine_rep + j, rep)
        block = lax.dynamic_index_in_dim(blocks, to, 0, keepdims=False)
        if piece:
            route = [
                (a * rep + b, ((a + i) % space) * rep + (b + j) % rep)
                for a in range(space)
                for b in range(rep)
            ]
            block = lax.ppermute(block, ("space", "rep"), route)
        received.append(block)
    return received


def total_over(value, axis):
    if lax.axis_size(axis) == 2:
        return value + from_behind(value, axis, 1)
    return lax.psum(value, axis)


def body(colour_vectors, gauge_links):
    local_count, _, _, local_z, local_x = colour_vectors.shape
    space = lax.axis_size("space")
    rep = lax.axis_size("rep")
    vec = lax.axis_size("vec")
    group = space * rep
    count = local_count // group
    planes = local_z * space
    width = local_x * rep
    shape = (6 * planes, count, width)

    own_links = gauge_links.reshape(6, 9, local_z, local_x).transpose(2, 0, 1, 3)
    links = []
    for i in range(space):
        plane_links = from_behind(own_links, "space", i)
        for j in range(rep):
            links.append(from_behind(plane_links, "rep", j))

    blocks = colour_vectors.reshape(group, count, 6, local_z, local_x).transpose(0, 2, 3, 1, 4)
    starts = exchange(blocks, space, rep)

    mine = lax.axis_index("space") * rep + lax.axis_index("rep")
    mine_space, mine_rep = lax.axis_index("space"), lax.axis_index("rep")

    def by_source(received):
        sources = []
        for source in range(group):
            i = lax.rem(mine_space + space - source // rep, space)
            j = lax.rem(mine_rep + rep - source % rep, rep)
            sources.append(lax.dynamic_index_in_dim(received, i * rep + j, 0, keepdims=False))
        return jnp.stack(sources)

    def home(field):
        field = field.reshape(6, space, local_z, count, rep, local_x)
        matrices = []
        for z in range(local_z):
            blocks = field[:, :, z].transpose(1, 3, 0, 2, 4).reshape(group, 6, count, local_x)
            blocks = by_source(jnp.stack(exchange(blocks, space, rep)))
            blocks = blocks.reshape(group, 2, 3, count, local_x).transpose(1, 0, 3, 2, 4)
            matrices.append(blocks.reshape(2 * local_count, 3 * local_x))
        return matrices

    whole_filtered = run_kernel(filter_kernel, starts, links, shape, space, rep, DEG)
    filtered = home(whole_filtered)
    whole_image = run_kernel(image_kernel, [whole_filtered], links, shape, space, rep, 1)
    position = lax.axis_index("vec")
    panels = [[matrix] for matrix in filtered]
    for distance in range(1, vec):
        route = [(p, p + 1) for p in range(distance - 1, vec - 1)]
        if distance == 1 and vec > 2:
            route = route[:-1]
        last = distance == vec - 1 and vec > 2
        if last:
            route = route + [(vec - 1, vec - 2)]
        for z in range(local_z):
            moving = panels[z][-1]
            if last:
                moving = jnp.where(position == vec - 1, filtered[z], moving)
            panels[z].append(lax.ppermute(moving, "vec", route))
    image = home(whole_image)

    out = jnp.stack(filtered).reshape(local_z, 2, local_count, 3, local_x).transpose(2, 1, 3, 0, 4)

    rows = jnp.zeros((2, 2, local_count, vec * local_count), jnp.float32)
    for distance in range(vec):
        product = 0.0
        for z in range(local_z):
            left = jnp.concatenate([filtered[z], image[z]], axis=0)
            product = product + inner_product(left, panels[z][distance])
        product = product.reshape(2, 2, local_count, 2, local_count)
        pair = jnp.stack(
            [
                product[:, 0, :, 0] + product[:, 1, :, 1],
                product[:, 0, :, 1] - product[:, 1, :, 0],
            ]
        )
        owner = lax.rem(position + vec - distance, vec)
        rows = lax.dynamic_update_slice(rows, pair, (0, 0, 0, owner * local_count))

    cut = rows.reshape(2, 2, local_count, vec, local_count).transpose(3, 0, 1, 2, 4)
    others = lax.all_to_all(cut, "vec", 0, 0)
    keep = (lax.broadcasted_iota(jnp.int32, (vec, 1, 1, 1, 1), 0) != position).astype(jnp.float32)
    others = (others * keep).transpose(1, 2, 4, 0, 3).reshape(rows.shape)
    rows = rows + others * jnp.array([1.0, -1.0], jnp.float32).reshape(2, 1, 1, 1)
    rows = total_over(total_over(rows, "rep"), "space") / float(width * planes)
    return (out, rows[:, 0], rows[:, 1])


def solution(mesh):
    return jax.shard_map(
        body,
        mesh=mesh,
        in_specs=(
            P(("cuts", "vec"), None, None, "space", "rep"),
            P(None, None, None, None, ("cuts", "space"), "rep"),
        ),
        out_specs=(
            P(("cuts", "vec"), None, None, "space", "rep"),
            P(None, ("cuts", "vec"), None),
            P(None, ("cuts", "vec"), None),
        ),
        check_vma=False,
    )
```

```python
import functools

import jax
import jax.numpy as jnp
from jax import lax
from jax.experimental import pallas as pl
from jax.experimental.pallas import tpu as pltpu
from jax.sharding import PartitionSpec as P

LX = 48
LY = 48
DEG = 8
LANES = 128


def shift_y(block, forward):
    width = block.shape[-1]
    position = lax.broadcasted_iota(jnp.int32, block.shape, 1) % LY
    if forward:
        return jnp.where(
            position == LY - 1,
            pltpu.roll(block, LY - 1, 1),
            pltpu.roll(block, width - 1, 1),
        )
    return jnp.where(
        position == 0, pltpu.roll(block, width - LY + 1, 1), pltpu.roll(block, 1, 1)
    )


def shift_x(block, forward):
    width = block.shape[-1]
    return pltpu.roll(block, width - LY if forward else LY, 1)


def piece_origin(piece, space, rep):
    i, j = piece // rep, piece % rep
    return (
        lax.rem(lax.axis_index("space") + space - i, space),
        lax.rem(lax.axis_index("rep") + rep - j, rep),
    )


def lane_block(index, size):
    return pl.ds(pl.multiple_of(index * size, LANES), size)


def prepare_links(pieces, made_ref, space, rep):
    local_z, _, _, local_x = pieces[0].shape
    for number, piece in enumerate(pieces):
        origin, half = piece_origin(number, space, rep)

        def place(z, carry, piece=piece, origin=origin, half=half):
            for mu in range(3):
                for part in range(2):
                    made_ref[origin * local_z + z, mu * 3 + part, :, lane_block(half, local_x)] = (
                        piece[z, mu * 2 + part]
                    )
            return carry

        lax.fori_loop(0, local_z, place, 0)

    def one(z, carry):
        for mu in range(3):
            real = made_ref[z, mu * 3]
            imag = made_ref[z, mu * 3 + 1]
            sources = [(mu, real, imag)]
            if mu == 0:
                sources.append((3, shift_x(real, False), shift_x(imag, False)))
            if mu == 1:
                sources.append((4, shift_y(real, False), shift_y(imag, False)))
            for slot, a, b in sources:
                made_ref[z, slot * 3] = a
                made_ref[z, slot * 3 + 1] = b - a
                made_ref[z, slot * 3 + 2] = a + b
        return carry

    lax.fori_loop(0, local_z * space, one, 0)


def hop_pass(source_ref, made_ref, moved_ref, planes, width, emit):
    def plane(z, carry):
        def move(comp, inner):
            field = source_ref[comp * planes + z]
            moved_ref[comp] = shift_x(field, True)
            moved_ref[6 + comp] = shift_y(field, True)
            moved_ref[12 + comp] = shift_x(field, False)
            moved_ref[18 + comp] = shift_y(field, False)
            return inner

        lax.fori_loop(0, 6, move, 0)
        ahead = lax.rem(z + 1, planes)
        behind = lax.rem(z + planes - 1, planes)

        def chunk(j, inner):
            lanes = pl.ds(pl.multiple_of(j * LANES, LANES), LANES)
            one = [None] * 3
            two = [None] * 3
            three = [None] * 3

            def add(total, term):
                return term if total is None else total + term

            def sub(total, term):
                return -term if total is None else total - term

            terms = (
                (0, z, lambda c: moved_ref[c, :, lanes], False),
                (1, z, lambda c: moved_ref[6 + c, :, lanes], False),
                (2, z, lambda c: source_ref[c * planes + ahead, :, lanes], False),
                (3, z, lambda c: moved_ref[12 + c, :, lanes], True),
                (4, z, lambda c: moved_ref[18 + c, :, lanes], True),
                (2, behind, lambda c: source_ref[c * planes + behind, :, lanes], True),
            )
            for slot, link_plane, load, dagger in terms:
                for col in range(3):
                    x = load(col)
                    y = load(3 + col)
                    both = x + y
                    for row in range(3):
                        entry = col * 3 + row if dagger else row * 3 + col
                        at = slice(entry, entry + 1)
                        a = made_ref[link_plane, slot * 3, at, lanes]
                        m = made_ref[link_plane, slot * 3 + 1, at, lanes]
                        p = made_ref[link_plane, slot * 3 + 2, at, lanes]
                        one[row] = add(one[row], a * both)
                        if dagger:
                            two[row] = sub(two[row], p * x)
                            three[row] = sub(three[row], m * y)
                        else:
                            two[row] = add(two[row], m * x)
                            three[row] = add(three[row], p * y)
            for row in range(3):
                emit(row * planes + z, lanes, one[row] - three[row])
                emit((3 + row) * planes + z, lanes, one[row] + two[row])
            return inner

        lax.fori_loop(0, width // LANES, chunk, 0, unroll=2)
        return carry

    lax.fori_loop(0, planes, plane, 0)


def filter_kernel(space, rep, *refs):
    group = space * rep
    starts, links = refs[:group], refs[group : 2 * group]
    out_ref, made_ref, fields_ref, moved_ref = refs[2 * group :]
    _, local_z, count, local_x = starts[0].shape
    planes = local_z * space
    width = local_x * rep
    prepare_links(links, made_ref, space, rep)

    for number, piece in enumerate(starts):
        origin, half = piece_origin(number, space, rep)

        def place(comp, carry, piece=piece, origin=origin, half=half):
            for z in range(local_z):
                at = comp * planes + origin * local_z + z
                block = piece[comp, z]
                fields_ref[0, at, :, lane_block(half, local_x)] = block
                fields_ref[1, at, :, lane_block(half, local_x)] = jnp.zeros_like(block)
            return carry

        lax.fori_loop(0, 6, place, 0)

    def step(k, carry):
        now = lax.rem(k, 2)
        later = 1 - now
        scale = jnp.where(k == 0, -1.0 / 11.0, -2.0 / 11.0).astype(jnp.float32)
        current = fields_ref.at[now]
        target = fields_ref.at[later]

        def emit(i, lanes, hop):
            target[i, :, lanes] = scale * (current[i, :, lanes] + 2.0 * hop) - target[i, :, lanes]

        hop_pass(current, made_ref, moved_ref, planes, width, emit)
        return carry

    lax.fori_loop(0, DEG, step, 0)

    def leave(i, carry):
        out_ref[i] = fields_ref[DEG % 2, i]
        return carry

    lax.fori_loop(0, 6 * planes, leave, 0)


def image_kernel(space, rep, *refs):
    group = space * rep
    field_ref, links = refs[0], refs[1 : 1 + group]
    out_ref, made_ref, moved_ref = refs[1 + group :]
    prepare_links(links, made_ref, space, rep)

    def emit(i, lanes, hop):
        out_ref[i, :, lanes] = 6.0 * field_ref[i, :, lanes] - hop

    hop_pass(field_ref, made_ref, moved_ref, field_ref.shape[0] // 6, field_ref.shape[2], emit)


def run_kernel(kernel, fields, links, shape, space, rep, hops):
    rows, count, width = shape
    scratch = [pltpu.VMEM((rows // 6, 15, 9, width), jnp.float32)]
    if hops > 1:
        scratch.append(pltpu.VMEM((2,) + shape, jnp.float32))
    scratch.append(pltpu.VMEM((24, count, width), jnp.float32))
    return pl.pallas_call(
        functools.partial(kernel, space, rep),
        out_shape=jax.ShapeDtypeStruct(shape, jnp.float32),
        in_specs=[pl.BlockSpec(memory_space=pltpu.VMEM)] * (len(fields) + len(links)),
        out_specs=pl.BlockSpec(memory_space=pltpu.VMEM),
        scratch_shapes=scratch,
        compiler_params=pltpu.CompilerParams(vmem_limit_bytes=62 * 1024 * 1024),
        cost_estimate=pl.CostEstimate(
            flops=hops * rows * count * width * 72, bytes_accessed=hops * 40_000_000, transcendentals=0
        ),
    )(*fields, *links)


def inner_product(left_matrix, right_matrix):
    return lax.dot_general(
        left_matrix,
        right_matrix,
        (((1,), (1,)), ((), ())),
        precision=lax.Precision.HIGH,
        preferred_element_type=jnp.float32,
    )


def from_behind(block, axis, distance):
    if distance == 0:
        return block
    count = lax.axis_size(axis)
    return lax.ppermute(block, axis, [(i, (i + distance) % count) for i in range(count)])


def exchange(blocks, space, rep):
    group = space * rep
    mine_space, mine_rep = lax.axis_index("space"), lax.axis_index("rep")
    received = []
    for piece in range(group):
        i, j = piece // rep, piece % rep
        to = lax.rem(mine_space + i, space) * rep + lax.rem(mine_rep + j, rep)
        block = lax.dynamic_index_in_dim(blocks, to, 0, keepdims=False)
        if piece:
            route = [
                (a * rep + b, ((a + i) % space) * rep + (b + j) % rep)
                for a in range(space)
                for b in range(rep)
            ]
            block = lax.ppermute(block, ("space", "rep"), route)
        received.append(block)
    return received


def total_over(value, axis):
    if lax.axis_size(axis) == 2:
        return value + from_behind(value, axis, 1)
    return lax.psum(value, axis)


def body(colour_vectors, gauge_links):
    local_count, _, _, local_z, local_x = colour_vectors.shape
    space = lax.axis_size("space")
    rep = lax.axis_size("rep")
    vec = lax.axis_size("vec")
    group = space * rep
    count = local_count // group
    planes = local_z * space
    width = local_x * rep
    shape = (6 * planes, count, width)

    own_links = gauge_links.reshape(6, 9, local_z, local_x).transpose(2, 0, 1, 3)
    links = []
    for i in range(space):
        plane_links = from_behind(own_links, "space", i)
        for j in range(rep):
            links.append(from_behind(plane_links, "rep", j))

    blocks = colour_vectors.reshape(group, count, 6, local_z, local_x).transpose(0, 2, 3, 1, 4)
    starts = exchange(blocks, space, rep)

    mine = lax.axis_index("space") * rep + lax.axis_index("rep")
    mine_space, mine_rep = lax.axis_index("space"), lax.axis_index("rep")

    def by_source(received):
        sources = []
        for source in range(group):
            i = lax.rem(mine_space + space - source // rep, space)
            j = lax.rem(mine_rep + rep - source % rep, rep)
            sources.append(lax.dynamic_index_in_dim(received, i * rep + j, 0, keepdims=False))
        return jnp.stack(sources)

    def home(field):
        field = field.reshape(6, space, local_z, count, rep, local_x)
        matrices = []
        for z in range(local_z):
            blocks = field[:, :, z].transpose(1, 3, 0, 2, 4).reshape(group, 6, count, local_x)
            blocks = by_source(jnp.stack(exchange(blocks, space, rep)))
            blocks = blocks.reshape(group, 2, 3, count, local_x).transpose(1, 0, 3, 2, 4)
            matrices.append(blocks.reshape(2 * local_count, 3 * local_x))
        return matrices

    whole_filtered = run_kernel(filter_kernel, starts, links, shape, space, rep, DEG)
    filtered = home(whole_filtered)
    panels = [[matrix] for matrix in filtered]
    whole_later, filtered = lax.optimization_barrier((whole_filtered, filtered))
    whole_image = run_kernel(image_kernel, [whole_later], links, shape, space, rep, 1)
    position = lax.axis_index("vec")
    for distance in range(1, vec):
        route = [(p, p + 1) for p in range(distance - 1, vec - 1)]
        if distance == 1 and vec > 2:
            route = route[:-1]
        last = distance == vec - 1 and vec > 2
        if last:
            route = route + [(vec - 1, vec - 2)]
        for z in range(local_z):
            moving = panels[z][-1]
            if last:
                moving = jnp.where(position == vec - 1, filtered[z], moving)
            panels[z].append(lax.ppermute(moving, "vec", route))
    image = home(whole_image)

    out = jnp.stack(filtered).reshape(local_z, 2, local_count, 3, local_x).transpose(2, 1, 3, 0, 4)

    rows = jnp.zeros((2, 2, local_count, vec * local_count), jnp.float32)
    for distance in range(vec):
        product = 0.0
        for z in range(local_z):
            left = jnp.concatenate([filtered[z], image[z]], axis=0)
            product = product + inner_product(left, panels[z][distance])
        product = product.reshape(2, 2, local_count, 2, local_count)
        pair = jnp.stack(
            [
                product[:, 0, :, 0] + product[:, 1, :, 1],
                product[:, 0, :, 1] - product[:, 1, :, 0],
            ]
        )
        owner = lax.rem(position + vec - distance, vec)
        rows = lax.dynamic_update_slice(rows, pair, (0, 0, 0, owner * local_count))

    cut = rows.reshape(2, 2, local_count, vec, local_count).transpose(3, 0, 1, 2, 4)
    others = lax.all_to_all(cut, "vec", 0, 0)
    keep = (lax.broadcasted_iota(jnp.int32, (vec, 1, 1, 1, 1), 0) != position).astype(jnp.float32)
    others = (others * keep).transpose(1, 2, 4, 0, 3).reshape(rows.shape)
    rows = rows + others * jnp.array([1.0, -1.0], jnp.float32).reshape(2, 1, 1, 1)
    rows = total_over(total_over(rows, "rep"), "space") / float(width * planes)
    return (out, rows[:, 0], rows[:, 1])


def solution(mesh):
    return jax.shard_map(
        body,
        mesh=mesh,
        in_specs=(
            P(("cuts", "vec"), None, None, "space", "rep"),
            P(None, None, None, None, ("cuts", "space"), "rep"),
        ),
        out_specs=(
            P(("cuts", "vec"), None, None, "space", "rep"),
            P(None, ("cuts", "vec"), None),
            P(None, ("cuts", "vec"), None),
        ),
        check_vma=False,
    )
```

```python
import functools

import jax
import jax.numpy as jnp
from jax import lax
from jax.experimental import pallas as pl
from jax.experimental.pallas import tpu as pltpu
from jax.sharding import PartitionSpec as P

LX = 48
LY = 48
DEG = 8
LANES = 128


def shift_y(block, forward):
    width = block.shape[-1]
    position = lax.broadcasted_iota(jnp.int32, block.shape, 1) % LY
    if forward:
        return jnp.where(
            position == LY - 1,
            pltpu.roll(block, LY - 1, 1),
            pltpu.roll(block, width - 1, 1),
        )
    return jnp.where(
        position == 0, pltpu.roll(block, width - LY + 1, 1), pltpu.roll(block, 1, 1)
    )


def shift_x(block, forward):
    width = block.shape[-1]
    return pltpu.roll(block, width - LY if forward else LY, 1)


def piece_origin(piece, space, rep):
    i, j = piece // rep, piece % rep
    return (
        lax.rem(lax.axis_index("space") + space - i, space),
        lax.rem(lax.axis_index("rep") + rep - j, rep),
    )


def lane_block(index, size):
    return pl.ds(pl.multiple_of(index * size, LANES), size)


def prepare_links(pieces, made_ref, space, rep):
    local_z, _, _, local_x = pieces[0].shape
    for number, piece in enumerate(pieces):
        origin, half = piece_origin(number, space, rep)

        def place(z, carry, piece=piece, origin=origin, half=half):
            for mu in range(3):
                for part in range(2):
                    made_ref[origin * local_z + z, mu * 3 + part, :, lane_block(half, local_x)] = (
                        piece[z, mu * 2 + part]
                    )
            return carry

        lax.fori_loop(0, local_z, place, 0)

    def one(z, carry):
        for mu in range(3):
            real = made_ref[z, mu * 3]
            imag = made_ref[z, mu * 3 + 1]
            sources = [(mu, real, imag)]
            if mu == 0:
                sources.append((3, shift_x(real, False), shift_x(imag, False)))
            if mu == 1:
                sources.append((4, shift_y(real, False), shift_y(imag, False)))
            for slot, a, b in sources:
                made_ref[z, slot * 3] = a
                made_ref[z, slot * 3 + 1] = b - a
                made_ref[z, slot * 3 + 2] = a + b
        return carry

    lax.fori_loop(0, local_z * space, one, 0)


def hop_pass(source_ref, made_ref, moved_ref, planes, width, emit):
    def plane(z, carry):
        def move(comp, inner):
            field = source_ref[comp * planes + z]
            moved_ref[comp] = shift_x(field, True)
            moved_ref[6 + comp] = shift_y(field, True)
            moved_ref[12 + comp] = shift_x(field, False)
            moved_ref[18 + comp] = shift_y(field, False)
            return inner

        lax.fori_loop(0, 6, move, 0)
        ahead = lax.rem(z + 1, planes)
        behind = lax.rem(z + planes - 1, planes)

        def chunk(j, inner):
            lanes = pl.ds(pl.multiple_of(j * LANES, LANES), LANES)
            one = [None] * 3
            two = [None] * 3
            three = [None] * 3

            def add(total, term):
                return term if total is None else total + term

            def sub(total, term):
                return -term if total is None else total - term

            terms = (
                (0, z, lambda c: moved_ref[c, :, lanes], False),
                (1, z, lambda c: moved_ref[6 + c, :, lanes], False),
                (2, z, lambda c: source_ref[c * planes + ahead, :, lanes], False),
                (3, z, lambda c: moved_ref[12 + c, :, lanes], True),
                (4, z, lambda c: moved_ref[18 + c, :, lanes], True),
                (2, behind, lambda c: source_ref[c * planes + behind, :, lanes], True),
            )
            for slot, link_plane, load, dagger in terms:
                for col in range(3):
                    x = load(col)
                    y = load(3 + col)
                    both = x + y
                    for row in range(3):
                        entry = col * 3 + row if dagger else row * 3 + col
                        at = slice(entry, entry + 1)
                        a = made_ref[link_plane, slot * 3, at, lanes]
                        m = made_ref[link_plane, slot * 3 + 1, at, lanes]
                        p = made_ref[link_plane, slot * 3 + 2, at, lanes]
                        one[row] = add(one[row], a * both)
                        if dagger:
                            two[row] = sub(two[row], p * x)
                            three[row] = sub(three[row], m * y)
                        else:
                            two[row] = add(two[row], m * x)
                            three[row] = add(three[row], p * y)
            for row in range(3):
                emit(row * planes + z, lanes, one[row] - three[row])
                emit((3 + row) * planes + z, lanes, one[row] + two[row])
            return inner

        lax.fori_loop(0, width // LANES, chunk, 0, unroll=2)
        return carry

    lax.fori_loop(0, planes, plane, 0)


def filter_kernel(space, rep, *refs):
    group = space * rep
    starts, links = refs[:group], refs[group : 2 * group]
    out_ref, made_ref, fields_ref, moved_ref = refs[2 * group :]
    _, local_z, count, local_x = starts[0].shape
    planes = local_z * space
    width = local_x * rep
    prepare_links(links, made_ref, space, rep)

    for number, piece in enumerate(starts):
        origin, half = piece_origin(number, space, rep)

        def place(comp, carry, piece=piece, origin=origin, half=half):
            for z in range(local_z):
                at = comp * planes + origin * local_z + z
                block = piece[comp, z]
                fields_ref[0, at, :, lane_block(half, local_x)] = block
                fields_ref[1, at, :, lane_block(half, local_x)] = jnp.zeros_like(block)
            return carry

        lax.fori_loop(0, 6, place, 0)

    def step(k, carry):
        now = lax.rem(k, 2)
        later = 1 - now
        scale = jnp.where(k == 0, -1.0 / 11.0, -2.0 / 11.0).astype(jnp.float32)
        current = fields_ref.at[now]
        target = fields_ref.at[later]

        def emit(i, lanes, hop):
            target[i, :, lanes] = scale * (current[i, :, lanes] + 2.0 * hop) - target[i, :, lanes]

        hop_pass(current, made_ref, moved_ref, planes, width, emit)
        return carry

    lax.fori_loop(0, DEG, step, 0)

    def leave(i, carry):
        out_ref[i] = fields_ref[DEG % 2, i]
        return carry

    lax.fori_loop(0, 6 * planes, leave, 0)


def image_kernel(space, rep, *refs):
    group = space * rep
    field_ref, links = refs[0], refs[1 : 1 + group]
    out_ref, made_ref, moved_ref = refs[1 + group :]
    prepare_links(links, made_ref, space, rep)

    def emit(i, lanes, hop):
        out_ref[i, :, lanes] = 6.0 * field_ref[i, :, lanes] - hop

    hop_pass(field_ref, made_ref, moved_ref, field_ref.shape[0] // 6, field_ref.shape[2], emit)


def run_kernel(kernel, fields, links, shape, space, rep, hops):
    rows, count, width = shape
    scratch = [pltpu.VMEM((rows // 6, 15, 9, width), jnp.float32)]
    if hops > 1:
        scratch.append(pltpu.VMEM((2,) + shape, jnp.float32))
    scratch.append(pltpu.VMEM((24, count, width), jnp.float32))
    return pl.pallas_call(
        functools.partial(kernel, space, rep),
        out_shape=jax.ShapeDtypeStruct(shape, jnp.float32),
        in_specs=[pl.BlockSpec(memory_space=pltpu.VMEM)] * (len(fields) + len(links)),
        out_specs=pl.BlockSpec(memory_space=pltpu.VMEM),
        scratch_shapes=scratch,
        compiler_params=pltpu.CompilerParams(vmem_limit_bytes=62 * 1024 * 1024),
        cost_estimate=pl.CostEstimate(
            flops=hops * rows * count * width * 72, bytes_accessed=hops * 40_000_000, transcendentals=0
        ),
    )(*fields, *links)


def inner_product(left_matrix, right_matrix):
    return lax.dot_general(
        left_matrix,
        right_matrix,
        (((1,), (1,)), ((), ())),
        precision=lax.Precision.HIGH,
        preferred_element_type=jnp.float32,
    )


def from_behind(block, axis, distance):
    if distance == 0:
        return block
    count = lax.axis_size(axis)
    return lax.ppermute(block, axis, [(i, (i + distance) % count) for i in range(count)])


def exchange(blocks, space, rep):
    group = space * rep
    mine_space, mine_rep = lax.axis_index("space"), lax.axis_index("rep")
    received = []
    for piece in range(group):
        i, j = piece // rep, piece % rep
        to = lax.rem(mine_space + i, space) * rep + lax.rem(mine_rep + j, rep)
        block = lax.dynamic_index_in_dim(blocks, to, 0, keepdims=False)
        if piece:
            route = [
                (a * rep + b, ((a + i) % space) * rep + (b + j) % rep)
                for a in range(space)
                for b in range(rep)
            ]
            block = lax.ppermute(block, ("space", "rep"), route)
        received.append(block)
    return received


def total_over(value, axis):
    if lax.axis_size(axis) == 2:
        return value + from_behind(value, axis, 1)
    return lax.psum(value, axis)


def body(colour_vectors, gauge_links):
    local_count, _, _, local_z, local_x = colour_vectors.shape
    space = lax.axis_size("space")
    rep = lax.axis_size("rep")
    vec = lax.axis_size("vec")
    group = space * rep
    count = local_count // group
    planes = local_z * space
    width = local_x * rep
    shape = (6 * planes, count, width)

    own_links = gauge_links.reshape(6, 9, local_z, local_x).transpose(2, 0, 1, 3)
    links = []
    for i in range(space):
        plane_links = from_behind(own_links, "space", i)
        for j in range(rep):
            links.append(from_behind(plane_links, "rep", j))

    blocks = colour_vectors.reshape(group, count, 6, local_z, local_x).transpose(0, 2, 3, 1, 4)
    starts = exchange(blocks, space, rep)

    mine = lax.axis_index("space") * rep + lax.axis_index("rep")
    mine_space, mine_rep = lax.axis_index("space"), lax.axis_index("rep")

    def by_source(received):
        sources = []
        for source in range(group):
            i = lax.rem(mine_space + space - source // rep, space)
            j = lax.rem(mine_rep + rep - source % rep, rep)
            sources.append(lax.dynamic_index_in_dim(received, i * rep + j, 0, keepdims=False))
        return jnp.stack(sources)

    def home(field):
        field = field.reshape(6, space, local_z, count, rep, local_x)
        matrices = []
        for z in range(local_z):
            blocks = field[:, :, z].transpose(1, 3, 0, 2, 4).reshape(group, 6, count, local_x)
            blocks = by_source(jnp.stack(exchange(blocks, space, rep)))
            blocks = blocks.reshape(group, 2, 3, count, local_x).transpose(1, 0, 3, 2, 4)
            matrices.append(blocks.reshape(2 * local_count, 3 * local_x))
        return matrices

    whole_filtered = run_kernel(filter_kernel, starts, links, shape, space, rep, DEG)
    filtered = home(whole_filtered)
    panels = [[matrix] for matrix in filtered]
    whole_later, filtered = lax.optimization_barrier((whole_filtered, filtered))
    whole_image = run_kernel(image_kernel, [whole_later], links, shape, space, rep, 1)
    image = home(whole_image)
    lefts = [jnp.concatenate([filtered[z], image[z]], axis=0) for z in range(local_z)]

    def multiply(distance):
        return sum(inner_product(lefts[z], panels[z][distance]) for z in range(local_z))

    products = []
    position = lax.axis_index("vec")
    for distance in range(1, vec):
        route = [(p, p + 1) for p in range(distance - 1, vec - 1)]
        if distance == 1 and vec > 2:
            route = route[:-1]
        last = distance == vec - 1 and vec > 2
        if last:
            route = route + [(vec - 1, vec - 2)]
        heads = [panels[z][-1] for z in range(local_z)]
        if last:
            products = [multiply(d) for d in range(distance - 1)]
            heads, products = lax.optimization_barrier((heads, products))
        for z in range(local_z):
            moving = heads[z]
            if last:
                moving = jnp.where(position == vec - 1, filtered[z], moving)
            panels[z].append(lax.ppermute(moving, "vec", route))

    out = jnp.stack(filtered).reshape(local_z, 2, local_count, 3, local_x).transpose(2, 1, 3, 0, 4)

    rows = jnp.zeros((2, 2, local_count, vec * local_count), jnp.float32)
    for distance in range(vec):
        product = products[distance] if distance < len(products) else multiply(distance)
        product = product.reshape(2, 2, local_count, 2, local_count)
        pair = jnp.stack(
            [
                product[:, 0, :, 0] + product[:, 1, :, 1],
                product[:, 0, :, 1] - product[:, 1, :, 0],
            ]
        )
        owner = lax.rem(position + vec - distance, vec)
        rows = lax.dynamic_update_slice(rows, pair, (0, 0, 0, owner * local_count))

    cut = rows.reshape(2, 2, local_count, vec, local_count).transpose(3, 0, 1, 2, 4)
    others = lax.all_to_all(cut, "vec", 0, 0)
    keep = (lax.broadcasted_iota(jnp.int32, (vec, 1, 1, 1, 1), 0) != position).astype(jnp.float32)
    others = (others * keep).transpose(1, 2, 4, 0, 3).reshape(rows.shape)
    rows = rows + others * jnp.array([1.0, -1.0], jnp.float32).reshape(2, 1, 1, 1)
    rows = total_over(total_over(rows, "rep"), "space") / float(width * planes)
    return (out, rows[:, 0], rows[:, 1])


def solution(mesh):
    return jax.shard_map(
        body,
        mesh=mesh,
        in_specs=(
            P(("cuts", "vec"), None, None, "space", "rep"),
            P(None, None, None, None, ("cuts", "space"), "rep"),
        ),
        out_specs=(
            P(("cuts", "vec"), None, None, "space", "rep"),
            P(None, ("cuts", "vec"), None),
            P(None, ("cuts", "vec"), None),
        ),
        check_vma=False,
    )
```
